512 devices in a mesh: row: 16 (over y, core), col: 32 (over z, x).
Axes of the slice: x: 4, y: 8, z: 8, core: 2. Of those that a mesh axis runs over, the one named last changes fastest.
Arguments:
- a_vals: bfloat16 [2, 32, 64, 5, 128, 128], P(None, 'row', 'col'), may hold values from -0.5 to 0.5
- a_off: int32 [2, 32, 64, 5], P(None, 'row', 'col'), may hold values from 0 to 8, as said below
- a_count: int32 [2, 32, 64], P(None, 'row', 'col'), may hold values from 1 to 5
- p_vals: bfloat16 [32, 64, 4, 128, 128], P('row', 'col'), may hold values from -1.1953125 to 1.1953125
Outputs:
- coarse: bfloat16 [2, 16, 32, 25, 128, 128], P(None, 'row', 'col')
The draws below stay inside these ranges and needn't reach their ends.
Inputs may be any that keep to these rules, and one draw needn't show every extreme that they name: Each row of a_off lists 5 different stencil positions of 0 to 8.
All inputs are finite; a program needn't handle non-finite values.
Results may differ from the reference program's by a relative error of at most 0.0049.
Values may be sent and summed in bfloat16 or wider, within the bound.
A program may use at most 64 MiB of HBM per device.

```python
import jax
import jax.numpy as jnp
import numpy as np
from jax import lax

B = 128
KA = 5
OPS = 2
NXF = 32
NYF = 64


def draw_a_off(key, part):
    scores = jax.random.randint(key, (OPS, NXF, NYF, 9), 0, 1 << 20) * 16 + jnp.arange(9, dtype=jnp.int32)
    return jnp.argsort(scores, axis=-1)[..., :KA].astype(jnp.int32)


def set_ends(array, rng, smallest, largest):
    spot = [jax.random.randint(jax.random.fold_in(rng, axis), (), 0, length) for axis, length in enumerate(array.shape)]
    main_axis = array.shape.index(max(array.shape))
    next_to = spot[:main_axis] + [(spot[main_axis] + 1) % array.shape[main_axis]] + spot[main_axis + 1:]
    return array.at[tuple(spot)].set(smallest).at[tuple(next_to)].set(largest)


def block_levels(key, shape, split, least, top_value):
    loudness = 1.0
    for dim, parts in split:
        steps = jax.random.uniform(jax.random.fold_in(jax.random.fold_in(key, 6), dim), (parts,), jnp.float32, least / len(split), top_value / len(split))
        loudness = loudness * jnp.repeat(jnp.exp(steps), shape[dim] // parts).reshape((-1,) + (1,) * (len(shape) - 1 - dim))
    return loudness


def centred(stream_key, shape, width, reach, shards=(), kind=jnp.bfloat16):
    entries = width * jax.random.normal(stream_key, shape, jnp.float32)
    if shards:
        entries = entries * block_levels(stream_key, shape, shards, -0.22, 0.18)
    return jnp.clip(entries, -reach, reach).astype(kind)


def setup_inputs(seed: int = 0) -> dict:
    streams_of = jax.random.split(jax.random.key(seed), 5)
    return {
        "a_vals": centred(streams_of[0], (OPS, NXF, NYF, KA, B, B), B ** -0.5, 0.5, ((1, 16), (2, 32))),
        "a_off": draw_a_off(jax.random.fold_in(streams_of[4], 71), 0),
        "a_count": set_ends(jax.random.randint(streams_of[2], (OPS, NXF, NYF), 1, KA + 1), jax.random.fold_in(streams_of[2], 1), 1, KA).astype(jnp.int32),
        "p_vals": centred(streams_of[3], (NXF, NYF, 4, B, B), 0.2, 1.1953125, ((0, 16), (1, 32))),
    }


def coarse_table():
    band_table = np.zeros((16, 9, 25), np.float32)
    windows = []
    for lag_x in range(-1, 3):
        for lag_y in range(-1, 3):
            place = (lag_x + 1) * 4 + (lag_y + 1)
            corner_x = 1 if lag_x in (-1, 2) else 0
            corner_y = 1 if lag_y in (-1, 2) else 0
            windows.append((lag_x, lag_y, 2 * corner_x + corner_y))
            for step_x in range(3):
                for step_y in range(3):
                    target = (lag_x // 2 + step_x + 1) * 5 + (lag_y // 2 + step_y + 1)
                    band_table[place, step_x * 3 + step_y, target] = 1.0
    return band_table, windows


def band_index(near, anchor, corner):
    return jnp.floor_divide(near, 2) + corner * (2 * jnp.remainder(near, 2) - 1) - jnp.floor_divide(anchor, 2) + 1


def fine_products(blocks, slot_offsets, counts, p_vals):
    width_x, width_y = p_vals.shape[0], p_vals.shape[1]
    slot_total = blocks.shape[2]
    alive = (jnp.arange(slot_total, dtype=jnp.int32)[None, None, :] < counts[:, :, None]).astype(jnp.bfloat16)
    masked = blocks * alive[..., None, None]

    def one_row(row_index):
        row_blocks = masked[row_index].astype(jnp.float32)
        offsets = slot_offsets[row_index]
        near_x = row_index + offsets // 3 - 1
        anchor_y = jnp.arange(width_y, dtype=jnp.int32)[:, None]
        near_y = anchor_y + offsets % 3 - 1
        running = jnp.zeros(row_blocks.shape[:1] + (9,) + row_blocks.shape[2:], jnp.float32)
        for quadrant in range(4):
            picked = p_vals[jnp.remainder(near_x, width_x), jnp.remainder(near_y, width_y), quadrant].astype(jnp.float32)
            partial_terms = jnp.einsum('ykab,ykbc->ykac', row_blocks, picked)
            band = band_index(near_x, row_index, quadrant // 2) * 3 + band_index(near_y, anchor_y, quadrant % 2)
            onehot = (band[..., None] == jnp.arange(9, dtype=jnp.int32)).astype(jnp.float32)
            running = running + jnp.einsum('ykac,ykn->ynac', partial_terms, onehot)
        return running.astype(jnp.bfloat16)

    return lax.map(one_row, jnp.arange(width_x, dtype=jnp.int32))


def coarse_products(fine_w, p_vals):
    band_table, windows = coarse_table()
    width_x, width_y = p_vals.shape[0], p_vals.shape[1]
    coarse_cols = 2 * jnp.arange(width_y // 2, dtype=jnp.int32)

    def one_row(coarse_row):
        p_rows = jnp.stack([p_vals[jnp.remainder(2 * coarse_row + lag_x, width_x), jnp.remainder(coarse_cols + lag_y, width_y), quadrant] for lag_x, lag_y, quadrant in windows], axis=1)
        w_rows = jnp.stack([fine_w[:, jnp.remainder(2 * coarse_row + lag_x, width_x), jnp.remainder(coarse_cols + lag_y, width_y)] for lag_x, lag_y, quadrant in windows], axis=2)
        partial_terms = jnp.einsum('yuab,syujac->syujbc', p_rows.astype(jnp.float32), w_rows.astype(jnp.float32))
        summed = jnp.einsum('syujbc,ujn->synbc', partial_terms, jnp.asarray(band_table, dtype=jnp.float32))
        return summed.astype(jnp.bfloat16)

    rows_out = lax.map(one_row, jnp.arange(width_x // 2, dtype=jnp.int32))
    return jnp.moveaxis(rows_out, 0, 1)


def reference(a_vals, a_off, a_count, p_vals):
    fine_w = jnp.stack([fine_products(a_vals[operator], a_off[operator], a_count[operator], p_vals) for operator in range(a_vals.shape[0])])
    return coarse_products(fine_w, p_vals)
```

```python
import jax
import jax.numpy as jnp
from jax import lax
from jax.experimental import pallas as pl
from jax.experimental.pallas import tpu as pltpu
from jax.sharding import PartitionSpec as P

MESH = pl.DeviceIdType.MESH
BF16 = jnp.bfloat16
F32 = jnp.float32

CORNER = {(-1, 0): 0, (-1, 1): 1, (0, 0): 1, (0, 1): 0, (1, 1): 0, (1, 2): 1}


def slot_table(a_off, a_count):
    slots = a_off.shape[-1]
    flip_x = jnp.array([1, -1], jnp.int32)[None, :, None, None]
    flip_y = jnp.array([1, -1], jnp.int32)[None, None, :, None]
    place = (flip_x * (a_off // 3 - 1) + 1) * 3 + flip_y * (a_off % 3 - 1) + 1
    number = jnp.arange(slots, dtype=jnp.int32)
    hit = (place[..., None] == jnp.arange(9, dtype=jnp.int32)) & (number < a_count[..., None])[..., None]
    table = jnp.min(jnp.where(hit, number[:, None], slots), axis=3)
    operators, rows, cols = table.shape[:3]
    table = jnp.moveaxis(table, 2, 0).reshape(cols, operators * rows, 9)
    return jnp.pad(table, ((0, 0), (0, 8 - operators * rows), (0, 128 - 9)))


def kernel(row_count, col_count, a_hbm, p_hbm, t_hbm, out_ref,
           p_win, a_own, a_one, a_two, slot_of, w_buf, lhs_t, own, prod, recv,
           local_sem, col_send, col_recv, row_send, row_recv, prod_send, prod_recv):
    r = lax.axis_index("row")
    c = lax.axis_index("col")
    rows = [lax.rem(r + row_count - 1, row_count), lax.rem(r + 1, row_count)]
    cols = [lax.rem(c + col_count - 1, col_count), lax.rem(c + 1, col_count)]
    first = lax.rem(r, 2)
    second = 1 - first
    size = p_hbm.shape[-1]

    def to_row(number):
        return {"row": lax.rem(r + 2 * number - 1 + row_count, row_count), "col": c}

    barrier = pltpu.get_barrier_semaphore()
    for side in range(2):
        pl.semaphore_signal(barrier, inc=1, device_id={"row": rows[side], "col": c}, device_id_type=MESH)
        pl.semaphore_signal(barrier, inc=1, device_id={"row": r, "col": cols[side]}, device_id_type=MESH)

    local = [
        pltpu.make_async_copy(p_hbm, p_win.at[1:3, 2:4], local_sem.at[0]),
        pltpu.make_async_copy(a_hbm, a_own.at[:, :, :, 0:5], local_sem.at[1]),
        pltpu.make_async_copy(t_hbm, slot_of.at[1:3], local_sem.at[2]),
    ]
    for copy in local:
        copy.start()
    pl.semaphore_wait(barrier, 4)

    def remote(src, dst, send, recv_s, device):
        return pltpu.make_async_remote_copy(
            src_ref=src, dst_ref=dst, send_sem=send, recv_sem=recv_s,
            device_id=device, device_id_type=MESH,
        )

    col_copies = [[], []]
    for side in range(2):
        device = {"row": r, "col": cols[side]}
        land = 1 - side
        near, far = side, 1 - side
        near_at = 1 if land == 0 else 4
        far_at = 0 if land == 0 else 5
        table_at = 0 if land == 0 else 3
        parts = [
            (t_hbm.at[near], slot_of.at[table_at]),
            (p_hbm.at[:, near], p_win.at[1:3, near_at]),
            (p_hbm.at[:, far], p_win.at[1:3, far_at]),
            (a_hbm.at[:, first, near], a_one.at[land, :, 0:5]),
            (a_hbm.at[:, second, near], a_two.at[land, :, 0:5]),
        ]
        for number, (src, dst) in enumerate(parts):
            col_copies[side].append(
                remote(src, dst, col_send.at[side, number], col_recv.at[land, number], device)
            )
    row_copies = [[], []]
    for number in range(2):
        device = to_row(number)
        row_at = 3 if number == 0 else 0
        parts = [(p_hbm.at[number], p_win.at[row_at, 2:4])]
        for at in (1, 4, 0, 5):
            parts.append((p_win.at[1 + number, at], p_win.at[row_at, at]))
        for part, (src, dst) in enumerate(parts):
            row_copies[number].append(
                remote(src, dst, row_send.at[number, part], row_recv.at[number, part], device)
            )

    for part in range(5):
        for side in range(2):
            col_copies[side][part].start()
        if part == 0:
            for number in range(2):
                row_copies[number][0].start()

    zero = jnp.zeros((size, size), BF16)
    for operator in range(2):
        for side in range(2):
            a_one[side, operator, 5] = zero
            a_two[side, operator, 5] = zero
            for number in range(2):
                a_own[operator, number, side, 5] = zero

    def wait_col(part):
        for side in range(2):
            col_copies[side][part].wait_recv()

    def wait_row(part):
        for number in range(2):
            row_copies[number][part].wait_recv()

    def fine_rows(number, column, load):
        flip_x = 1 - 2 * number
        flip_y = 2 * lax.rem(column, 2) - 1

        def p_block(off_x, off_y, corner_x, corner_y):
            return p_win[number + 1 + flip_x * off_x, column + 1 + flip_y * off_y, 2 * corner_x + corner_y]

        for place_x in range(3):
            offs_x = [off for off in (-1, 0, 1) if (off, place_x) in CORNER]
            results = []
            for offs_y, places_y in (((-1, 0), (0, 1)), ((1,), (1, 2))):
                pairs = [(off_x, off_y) for off_x in offs_x for off_y in offs_y]
                left = jnp.concatenate(
                    [
                        jnp.concatenate(
                            [load(operator, (off_x + 1) * 3 + off_y + 1) for operator in range(2)], axis=0
                        )
                        for off_x, off_y in pairs
                    ],
                    axis=1,
                )
                right = jnp.concatenate(
                    [
                        jnp.concatenate(
                            [
                                p_block(off_x, off_y, CORNER[off_x, place_x], CORNER[off_y, place_y])
                                for place_y in places_y
                            ],
                            axis=1,
                        )
                        for off_x, off_y in pairs
                    ],
                    axis=0,
                )
                results.append(jnp.dot(left, right, preferred_element_type=F32))
            low, high = results
            columns = [low[:, :size], low[:, size:] + high[:, :size], high[:, size:]]
            for place_y in range(3):
                for operator in range(2):
                    w_buf[number, column, 1 + flip_x * (place_x - 1), 1 + flip_y * (place_y - 1), operator] = (
                        columns[place_y][operator * size : (operator + 1) * size].astype(BF16)
                    )

    def transposes(number, columns):
        for column in columns:
            corner_y = 1 if column in (0, 3) else 0
            for corner_x in range(2):
                lhs_t[number, corner_x * size : (corner_x + 1) * size, column * size : (column + 1) * size] = p_win[
                    1 + number, column + 1, 2 * corner_x + corner_y
                ].T

    def products(number, place_x, start):
        for place_n in range(5):
            low = [0, 0, 0, 1, 3][place_n]
            high = [1, 3, 4, 4, 4][place_n]
            right = jnp.concatenate(
                [
                    jnp.concatenate(
                        [
                            w_buf[number, column, place_x, place_n - [0, 1, 1, 2][column], operator]
                            for operator in range(2)
                        ],
                        axis=1,
                    )
                    for column in range(low, high)
                ],
                axis=0,
            )
            left = lhs_t[number, :, low * size : high * size]
            result = jnp.dot(left, right, preferred_element_type=F32)
            for operator in range(2):
                lanes = slice(operator * size, (operator + 1) * size)
                if start:
                    own[place_x, place_n, operator] = result[:size, lanes]
                else:
                    own[place_x, place_n, operator] += result[:size, lanes]
                prod[number, place_x, place_n, operator] = result[size:, lanes].astype(BF16)

    def halo_row(number, halo):
        @pl.loop(0, 2)
        def _(side):
            def load(operator, place):
                return halo[side, operator, slot_of[3 * side, operator * 2 + number, place]]

            fine_rows(number, 3 * side, load)

    wait_col(1)
    for number in range(2):
        row_copies[number][1].start()
        row_copies[number][2].start()
    for copy in local:
        copy.wait()
    for number in range(2):
        transposes(number, range(4))
    wait_row(0)
    wait_row(1)
    wait_row(2)

    @pl.loop(0, 4)
    def _(step):
        number = step // 2
        column = lax.rem(step, 2)

        def load(operator, place):
            return a_own[operator, number, column, slot_of[1 + column, operator * 2 + number, place]]

        fine_rows(number, 1 + column, load)

    wait_col(2)
    for number in range(2):
        row_copies[number][3].start()
        row_copies[number][4].start()
    wait_col(0)
    wait_col(3)
    wait_row(3)
    wait_row(4)

    prod_copies = []

    def send(number, order):
        def at(place_x):
            copy = remote(
                prod.at[number, place_x], recv.at[number, place_x],
                prod_send.at[order, place_x], prod_recv.at[number, place_x], to_row(number),
            )
            copy.start()
            prod_copies.append(copy)
        return at

    for order, (number, halo) in enumerate(((first, a_one), (second, a_two))):
        if order == 1:
            wait_col(4)
        halo_row(number, halo)
        push = send(number, order)
        for place_x in range(3):
            products(number, place_x, order == 0)
            push(place_x)

    for copy in prod_copies:
        copy.wait_recv()

    @pl.loop(0, 5)
    def _(place_n):
        for operator in range(2):
            for place in range(5):
                total = None
                if 1 <= place <= 3:
                    total = own[place - 1, place_n, operator]
                if place >= 2:
                    term = recv[0, place - 2, place_n, operator].astype(F32)
                    total = term if total is None else total + term
                if place <= 2:
                    term = recv[1, place, place_n, operator].astype(F32)
                    total = term if total is None else total + term
                out_ref[operator, place, place_n] = total.astype(BF16)

    for copies in col_copies + row_copies + [prod_copies]:
        for copy in copies:
            copy.wait_send()


def per_device(a_vals, a_off, a_count, p_vals):
    operators, size = a_vals.shape[0], a_vals.shape[-1]
    table = slot_table(a_off, a_count)
    rows, cols = lax.axis_size("row"), lax.axis_size("col")

    def body(*refs):
        kernel(rows, cols, *refs)

    block = (size, size)
    result = pl.pallas_call(
        body,
        out_shape=jax.ShapeDtypeStruct((operators, 5, 5) + block, BF16),
        in_specs=[pl.BlockSpec(memory_space=pl.ANY)] * 3,
        out_specs=pl.BlockSpec(memory_space=pltpu.VMEM),
        scratch_shapes=[
            pltpu.VMEM((4, 6, 4) + block, BF16),
            pltpu.VMEM((2, 2, 2, 6) + block, BF16),
            pltpu.VMEM((2, 2, 6) + block, BF16),
            pltpu.VMEM((2, 2, 6) + block, BF16),
            pltpu.SMEM((4, 8, 128), jnp.int32),
            pltpu.VMEM((2, 4, 3, 3, 2) + block, BF16),
            pltpu.VMEM((2, 2 * size, 4 * size), BF16),
            pltpu.VMEM((3, 5, 2) + block, F32),
            pltpu.VMEM((2, 3, 5, 2) + block, BF16),
            pltpu.VMEM((2, 3, 5, 2) + block, BF16),
            pltpu.SemaphoreType.DMA((3,)),
            pltpu.SemaphoreType.DMA((2, 5)),
            pltpu.SemaphoreType.DMA((2, 5)),
            pltpu.SemaphoreType.DMA((2, 5)),
            pltpu.SemaphoreType.DMA((2, 5)),
            pltpu.SemaphoreType.DMA((2, 3)),
            pltpu.SemaphoreType.DMA((2, 3)),
        ],
        compiler_params=pltpu.CompilerParams(
            collective_id=0, has_side_effects=True, vmem_limit_bytes=48 * 1024 * 1024
        ),
        name="galerkin",
    )(a_vals, p_vals, table)
    return result.reshape((operators, 1, 1, 25) + block)


def solution(mesh):
    placed = (
        P(None, "row", "col", None, None, None),
        P(None, "row", "col", None),
        P(None, "row", "col"),
        P("row", "col", None, None, None),
    )
    return jax.shard_map(
        per_device,
        mesh=mesh,
        in_specs=placed,
        out_specs=P(None, "row", "col", None, None, None),
        check_vma=False,
    )
```

```python
import jax
import jax.numpy as jnp
from jax import lax
from jax.experimental import pallas as pl
from jax.experimental.pallas import tpu as pltpu
from jax.sharding import PartitionSpec as P

MESH = pl.DeviceIdType.MESH
BF16 = jnp.bfloat16
F32 = jnp.float32

CORNER = {(-1, 0): 0, (-1, 1): 1, (0, 0): 1, (0, 1): 0, (1, 1): 0, (1, 2): 1}


def kernel(row_count, col_count, a_hbm, p_hbm, off_hbm, count_hbm, out_ref,
           p_win, a_own, a_half_0, a_half_1, a_half_2, a_half_3,
           off_ref, count_ref, off_halo, count_halo, slot_of,
           w_buf, lhs_t, own, prod, recv,
           local_sem, col_send, col_recv, row_send, row_recv, prod_send, prod_recv):
    r = lax.axis_index("row")
    c = lax.axis_index("col")
    rows = [lax.rem(r + row_count - 1, row_count), lax.rem(r + 1, row_count)]
    cols = [lax.rem(c + col_count - 1, col_count), lax.rem(c + 1, col_count)]
    first = lax.rem(r, 2)
    order = (first, 1 - first)
    halves = ((a_half_0, a_half_1), (a_half_2, a_half_3))
    size = p_hbm.shape[-1]
    slots = a_hbm.shape[3]

    def to_row(number):
        return {"row": lax.rem(r + 2 * number - 1 + row_count, row_count), "col": c}

    barrier = pltpu.get_barrier_semaphore()
    for side in range(2):
        pl.semaphore_signal(barrier, inc=1, device_id={"row": rows[side], "col": c}, device_id_type=MESH)
        pl.semaphore_signal(barrier, inc=1, device_id={"row": r, "col": cols[side]}, device_id_type=MESH)

    local = [
        pltpu.make_async_copy(p_hbm, p_win.at[1:3, 2:4], local_sem.at[0]),
        pltpu.make_async_copy(a_hbm, a_own.at[:, :, :, 0:slots], local_sem.at[1]),
        pltpu.make_async_copy(off_hbm, off_ref, local_sem.at[2]),
        pltpu.make_async_copy(count_hbm, count_ref, local_sem.at[3]),
    ]
    for copy in local:
        copy.start()
    pl.semaphore_wait(barrier, 4)

    def remote(src, dst, send, recv_s, device):
        return pltpu.make_async_remote_copy(
            src_ref=src, dst_ref=dst, send_sem=send, recv_sem=recv_s,
            device_id=device, device_id_type=MESH,
        )

    col_copies = [[], []]
    for side in range(2):
        device = {"row": r, "col": cols[side]}
        land = 1 - side
        near = side
        at = 0 if land == 0 else 4
        parts = [(p_hbm.at[number], p_win.at[1 + number, at : at + 2]) for number in order]
        for turn in range(2):
            for operator in range(2):
                parts.append(
                    (a_hbm.at[operator, order[turn], near], halves[turn][operator].at[land, 0:slots])
                )
        parts.append((off_hbm, off_halo.at[land]))
        parts.append((count_hbm, count_halo.at[land]))
        for part, (src, dst) in enumerate(parts):
            col_copies[side].append(
                remote(src, dst, col_send.at[side, part], col_recv.at[land, part], device)
            )
    row_copies = [[], []]
    for turn in range(2):
        number = order[turn]
        row_at = 3 * (1 - number)
        parts = [(p_hbm.at[number], p_win.at[row_at, 2:4])]
        for at in (0, 4):
            parts.append((p_win.at[1 + number, at : at + 2], p_win.at[row_at, at : at + 2]))
        for part, (src, dst) in enumerate(parts):
            row_copies[turn].append(
                remote(src, dst, row_send.at[turn, part], row_recv.at[number, part], to_row(number))
            )

    def start_col(part):
        for side in range(2):
            col_copies[side][part].start()

    def wait_col(part):
        for side in range(2):
            col_copies[side][part].wait_recv()

    for part in (6, 7, 0):
        start_col(part)
    for turn in range(2):
        row_copies[turn][0].start()
    for part in (1, 2, 3, 4, 5):
        start_col(part)

    zero = jnp.zeros((size, size), BF16)
    for operator in range(2):
        for side in range(2):
            for turn in range(2):
                halves[turn][operator][side, slots] = zero
                a_own[operator, turn, side, slots] = zero

    def table(column, off_at, count_at):
        @pl.loop(0, 4)
        def _(line):
            operator = line // 2
            number = lax.rem(line, 2)
            flip_x = 1 - 2 * number
            flip_y = 2 * (column % 2) - 1
            count = count_at(operator, number)
            places = []
            for slot in range(slots):
                off = off_at(operator, number, slot)
                off_x = (off >= 3).astype(jnp.int32) + (off >= 6).astype(jnp.int32)
                off_y = off - 3 * off_x
                place = 3 * (flip_x * (off_x - 1) + 1) + flip_y * (off_y - 1) + 1
                places.append(jnp.where(slot < count, place, -1))
            for position in range(9):
                found = jnp.int32(slots)
                for slot in range(slots):
                    found = jnp.where(places[slot] == position, slot, found)
                slot_of[column, line, position] = found

    def halo_table(side):
        table(
            3 * side,
            lambda operator, number, slot: off_halo[side, operator, number, 1 - side, slot],
            lambda operator, number: count_halo[side, operator, number, 1 - side],
        )

    def fine_rows(number, column, operators, load):
        flip_x = 1 - 2 * number
        flip_y = 2 * lax.rem(column, 2) - 1

        def p_block(off_x, off_y, corner_x, corner_y):
            return p_win[number + 1 + flip_x * off_x, column + 1 + flip_y * off_y, 2 * corner_x + corner_y]

        for place_x in range(3):
            offs_x = [off for off in (-1, 0, 1) if (off, place_x) in CORNER]
            results = []
            for offs_y, places_y in (((-1, 0), (0, 1)), ((1,), (1, 2))):
                pairs = [(off_x, off_y) for off_x in offs_x for off_y in offs_y]
                left = jnp.concatenate(
                    [
                        jnp.concatenate(
                            [load(operator, (off_x + 1) * 3 + off_y + 1) for operator in operators], axis=0
                        )
                        for off_x, off_y in pairs
                    ],
                    axis=1,
                )
                right = jnp.concatenate(
                    [
                        jnp.concatenate(
                            [
                                p_block(off_x, off_y, CORNER[off_x, place_x], CORNER[off_y, place_y])
                                for place_y in places_y
                            ],
                            axis=1,
                        )
                        for off_x, off_y in pairs
                    ],
                    axis=0,
                )
                results.append(jnp.dot(left, right, preferred_element_type=F32))
            low, high = results
            columns = [low[:, :size], low[:, size:] + high[:, :size], high[:, size:]]
            for place_y in range(3):
                for at, operator in enumerate(operators):
                    w_buf[operator, number, column, 1 + flip_x * (place_x - 1), 1 + flip_y * (place_y - 1)] = (
                        columns[place_y][at * size : (at + 1) * size].astype(BF16)
                    )

    def transposes(number):
        for column in range(4):
            corner_y = 1 if column in (0, 3) else 0
            for corner_x in range(2):
                lhs_t[number, corner_x * size : (corner_x + 1) * size, column * size : (column + 1) * size] = p_win[
                    1 + number, column + 1, 2 * corner_x + corner_y
                ].T

    def products(operator, number, places, start):
        for place_n in range(5):
            low = [0, 0, 0, 1, 3][place_n]
            high = [1, 3, 4, 4, 4][place_n]
            right = jnp.concatenate(
                [
                    jnp.concatenate(
                        [
                            w_buf[operator, number, column, place_x, place_n - [0, 1, 1, 2][column]]
                            for place_x in places
                        ],
                        axis=1,
                    )
                    for column in range(low, high)
                ],
                axis=0,
            )
            left = lhs_t[number, :, low * size : high * size]
            result = jnp.dot(left, right, preferred_element_type=F32)
            for at, place_x in enumerate(places):
                lanes = slice(at * size, (at + 1) * size)
                if start:
                    own[operator, place_x, place_n] = result[:size, lanes]
                else:
                    own[operator, place_x, place_n] += result[:size, lanes]
                prod[operator, number, place_x, place_n] = result[size:, lanes].astype(BF16)

    def own_row(number):
        @pl.loop(0, 2)
        def _(column):
            def load(operator, place):
                return a_own[operator, number, column, slot_of[1 + column, operator * 2 + number, place]]

            fine_rows(number, 1 + column, (0, 1), load)

    for copy in local:
        copy.wait()
    for column in (1, 2):
        table(
            column,
            lambda operator, number, slot, column=column: off_ref[operator, number, column - 1, slot],
            lambda operator, number, column=column: count_ref[operator, number, column - 1],
        )
    wait_col(6)
    wait_col(7)
    for side in range(2):
        halo_table(side)
    for turn in range(2):
        wait_col(turn)
        for part in (1, 2):
            row_copies[turn][part].start()
        transposes(order[turn])
    for copies in row_copies:
        for copy in copies:
            copy.wait_recv()

    prod_copies = [[], []]
    for turn in range(2):
        number = order[turn]
        own_row(number)
        for operator in range(2):
            half = halves[turn][operator]
            wait_col(2 + 2 * turn + operator)

            @pl.loop(0, 2)
            def _(side):
                def load(operator, place):
                    return half[side, slot_of[3 * side, operator * 2 + number, place]]

                fine_rows(number, 3 * side, (operator,), load)

            for piece, places in enumerate(((0, 1), (2,))):
                products(operator, number, places, turn == 0)
                part = slice(places[0], places[-1] + 1)
                copy = remote(
                    prod.at[operator, number, part], recv.at[operator, number, part],
                    prod_send.at[operator, turn, piece], prod_recv.at[operator, number, piece], to_row(number),
                )
                copy.start()
                prod_copies[operator].append(copy)

    for operator in range(2):
        for copy in prod_copies[operator]:
            copy.wait_recv()

        @pl.loop(0, 5)
        def _(place_n):
            for place in range(5):
                total = None
                if 1 <= place <= 3:
                    total = own[operator, place - 1, place_n]
                if place >= 2:
                    term = recv[operator, 0, place - 2, place_n].astype(F32)
                    total = term if total is None else total + term
                if place <= 2:
                    term = recv[operator, 1, place, place_n].astype(F32)
                    total = term if total is None else total + term
                out_ref[operator, place, place_n] = total.astype(BF16)

    for copies in col_copies + row_copies + prod_copies:
        for copy in copies:
            copy.wait_send()


def per_device(a_vals, a_off, a_count, p_vals):
    operators, size = a_vals.shape[0], a_vals.shape[-1]
    slots = a_vals.shape[3]
    rows, cols = lax.axis_size("row"), lax.axis_size("col")

    def body(*refs):
        kernel(rows, cols, *refs)

    block = (size, size)
    in_hbm = pl.BlockSpec(memory_space=pl.ANY)
    result = pl.pallas_call(
        body,
        out_shape=jax.ShapeDtypeStruct((operators, 5, 5) + block, BF16),
        in_specs=[in_hbm] * 4,
        out_specs=pl.BlockSpec(memory_space=pltpu.VMEM),
        scratch_shapes=[
            pltpu.VMEM((4, 6, 4) + block, BF16),
            pltpu.VMEM((2, 2, 2, slots + 1) + block, BF16),
        ]
        + [pltpu.VMEM((2, slots + 1) + block, BF16)] * 4
        + [
            pltpu.SMEM(a_off.shape, jnp.int32),
            pltpu.SMEM(a_count.shape, jnp.int32),
            pltpu.SMEM((2,) + a_off.shape, jnp.int32),
            pltpu.SMEM((2,) + a_count.shape, jnp.int32),
            pltpu.SMEM((4, 8, 128), jnp.int32),
            pltpu.VMEM((2, 2, 4, 3, 3) + block, BF16),
            pltpu.VMEM((2, 2 * size, 4 * size), BF16),
            pltpu.VMEM((2, 3, 5) + block, F32),
            pltpu.VMEM((2, 2, 3, 5) + block, BF16),
            pltpu.VMEM((2, 2, 3, 5) + block, BF16),
            pltpu.SemaphoreType.DMA((4,)),
            pltpu.SemaphoreType.DMA((2, 8)),
            pltpu.SemaphoreType.DMA((2, 8)),
            pltpu.SemaphoreType.DMA((2, 3)),
            pltpu.SemaphoreType.DMA((2, 3)),
            pltpu.SemaphoreType.DMA((2, 2, 2)),
            pltpu.SemaphoreType.DMA((2, 2, 2)),
        ],
        compiler_params=pltpu.CompilerParams(
            collective_id=0, has_side_effects=True, vmem_limit_bytes=48 * 1024 * 1024
        ),
        name="galerkin",
    )(*[pltpu.with_memory_space_constraint(array, pltpu.HBM) for array in (a_vals, p_vals, a_off, a_count)])
    return result.reshape((operators, 1, 1, 25) + block)


def solution(mesh):
    placed = (
        P(None, "row", "col", None, None, None),
        P(None, "row", "col", None),
        P(None, "row", "col"),
        P("row", "col", None, None, None),
    )
    return jax.shard_map(
        per_device,
        mesh=mesh,
        in_specs=placed,
        out_specs=P(None, "row", "col", None, None, None),
        check_vma=False,
    )
```

```python
import jax
import jax.numpy as jnp
from jax import lax
from jax.experimental import pallas as pl
from jax.experimental.pallas import tpu as pltpu
from jax.sharding import PartitionSpec as P

MESH = pl.DeviceIdType.MESH
BF16 = jnp.bfloat16
F32 = jnp.float32

CORNER = {(-1, 0): 0, (-1, 1): 1, (0, 0): 1, (0, 1): 0, (1, 1): 0, (1, 2): 1}


def kernel(row_count, col_count, a_hbm, p_hbm, off_hbm, count_hbm, out_ref,
           p_win, a_own, a_0, a_1, a_2, a_3, a_4, a_5, a_6, a_7,
           off_ref, count_ref, off_halo, count_halo, slot_of,
           w_buf, lhs_t, own, prod, recv,
           local_sem, col_send, col_recv, row_send, row_recv, prod_send, prod_recv):
    r = lax.axis_index("row")
    c = lax.axis_index("col")
    rows = [lax.rem(r + row_count - 1, row_count), lax.rem(r + 1, row_count)]
    cols = [lax.rem(c + col_count - 1, col_count), lax.rem(c + 1, col_count)]
    first = lax.rem(r, 2)
    order = (first, 1 - first)
    halves = (((a_0, a_1), (a_2, a_3)), ((a_4, a_5), (a_6, a_7)))
    size = p_hbm.shape[-1]
    slots = a_hbm.shape[3]

    def to_row(number):
        return {"row": lax.rem(r + 2 * number - 1 + row_count, row_count), "col": c}

    barrier = pltpu.get_barrier_semaphore()
    for side in range(2):
        pl.semaphore_signal(barrier, inc=1, device_id={"row": rows[side], "col": c}, device_id_type=MESH)
        pl.semaphore_signal(barrier, inc=1, device_id={"row": r, "col": cols[side]}, device_id_type=MESH)

    local = [
        pltpu.make_async_copy(p_hbm, p_win.at[1:3, 2:4], local_sem.at[0]),
        pltpu.make_async_copy(a_hbm, a_own.at[:, :, :, 0:slots], local_sem.at[1]),
        pltpu.make_async_copy(off_hbm, off_ref, local_sem.at[2]),
        pltpu.make_async_copy(count_hbm, count_ref, local_sem.at[3]),
    ]
    for copy in local:
        copy.start()
    pl.semaphore_wait(barrier, 4)

    def remote(src, dst, send, recv_s, device):
        return pltpu.make_async_remote_copy(
            src_ref=src, dst_ref=dst, send_sem=send, recv_sem=recv_s,
            device_id=device, device_id_type=MESH,
        )

    col_copies = [[], []]
    for side in range(2):
        device = {"row": r, "col": cols[side]}
        land = 1 - side
        near = side
        at = 0 if land == 0 else 4
        parts = [(p_hbm.at[number], p_win.at[1 + number, at : at + 2]) for number in order]
        for turn in range(2):
            for operator in range(2):
                parts.append(
                    (a_hbm.at[operator, order[turn], near], halves[turn][operator][land].at[0:slots])
                )
        parts.append((off_hbm, off_halo.at[land]))
        parts.append((count_hbm, count_halo.at[land]))
        for part, (src, dst) in enumerate(parts):
            col_copies[side].append(
                remote(src, dst, col_send.at[side, part], col_recv.at[land, part], device)
            )
    row_copies = [[], []]
    for turn in range(2):
        number = order[turn]
        row_at = 3 * (1 - number)
        parts = [(p_hbm.at[number], p_win.at[row_at, 2:4])]
        for at in (0, 4):
            parts.append((p_win.at[1 + number, at : at + 2], p_win.at[row_at, at : at + 2]))
        for part, (src, dst) in enumerate(parts):
            row_copies[turn].append(
                remote(src, dst, row_send.at[turn, part], row_recv.at[number, part], to_row(number))
            )

    def start_col(part):
        for side in range(2):
            col_copies[side][part].start()

    def wait_col(part, sides=(0, 1)):
        for side in sides:
            col_copies[1 - side][part].wait_recv()

    start_col(0)
    for turn in range(2):
        row_copies[turn][0].start()
    for part in (6, 7, 1, 2, 3, 4, 5):
        start_col(part)

    zero = jnp.zeros((size, size), BF16)
    for operator in range(2):
        for side in range(2):
            for turn in range(2):
                halves[turn][operator][side][slots] = zero
                a_own[operator, turn, side, slots] = zero

    def table(column, off_at, count_at):
        @pl.loop(0, 4)
        def _(line):
            operator = line // 2
            number = lax.rem(line, 2)
            flip_x = 1 - 2 * number
            flip_y = 2 * (column % 2) - 1
            count = count_at(operator, number)
            places = []
            for slot in range(slots):
                off = off_at(operator, number, slot)
                off_x = (off >= 3).astype(jnp.int32) + (off >= 6).astype(jnp.int32)
                off_y = off - 3 * off_x
                place = 3 * (flip_x * (off_x - 1) + 1) + flip_y * (off_y - 1) + 1
                places.append(jnp.where(slot < count, place, -1))
            for position in range(9):
                found = jnp.int32(slots)
                for slot in range(slots):
                    found = jnp.where(places[slot] == position, slot, found)
                slot_of[column, line, position] = found

    def halo_table(side):
        table(
            3 * side,
            lambda operator, number, slot: off_halo[side, operator, number, 1 - side, slot],
            lambda operator, number: count_halo[side, operator, number, 1 - side],
        )

    def fine_rows(number, column, operators, load):
        flip_x = 1 - 2 * number
        flip_y = 2 * (column % 2) - 1

        def p_block(off_x, off_y, corner_x, corner_y):
            return p_win[number + 1 + flip_x * off_x, column + 1 + flip_y * off_y, 2 * corner_x + corner_y]

        for place_x in range(3):
            offs_x = [off for off in (-1, 0, 1) if (off, place_x) in CORNER]
            results = []
            for offs_y, places_y in (((-1, 0), (0, 1)), ((1,), (1, 2))):
                pairs = [(off_x, off_y) for off_x in offs_x for off_y in offs_y]
                left = jnp.concatenate(
                    [
                        jnp.concatenate(
                            [load(operator, (off_x + 1) * 3 + off_y + 1) for operator in operators], axis=0
                        )
                        for off_x, off_y in pairs
                    ],
                    axis=1,
                )
                right = jnp.concatenate(
                    [
                        jnp.concatenate(
                            [
                                p_block(off_x, off_y, CORNER[off_x, place_x], CORNER[off_y, place_y])
                                for place_y in places_y
                            ],
                            axis=1,
                        )
                        for off_x, off_y in pairs
                    ],
                    axis=0,
                )
                results.append(jnp.dot(left, right, preferred_element_type=F32))
            low, high = results
            columns = [low[:, :size], low[:, size:] + high[:, :size], high[:, size:]]
            for place_y in range(3):
                for at, operator in enumerate(operators):
                    w_buf[operator, number, column, 1 + flip_x * (place_x - 1), 1 + flip_y * (place_y - 1)] = (
                        columns[place_y][at * size : (at + 1) * size].astype(BF16)
                    )

    def transposes(number):
        for column in range(4):
            corner_y = 1 if column in (0, 3) else 0
            for corner_x in range(2):
                lhs_t[number, corner_x * size : (corner_x + 1) * size, column * size : (column + 1) * size] = p_win[
                    1 + number, column + 1, 2 * corner_x + corner_y
                ].T

    def products(operator, number, place_ns, start):
        for place_n in place_ns:
            low = [0, 0, 0, 1, 3][place_n]
            high = [1, 3, 4, 4, 4][place_n]
            left = lhs_t[number, :, low * size : high * size]
            for places in ((0, 1), (2,)):
                right = jnp.concatenate(
                    [
                        jnp.concatenate(
                            [
                                w_buf[operator, number, column, place_x, place_n - [0, 1, 1, 2][column]]
                                for place_x in places
                            ],
                            axis=1,
                        )
                        for column in range(low, high)
                    ],
                    axis=0,
                )
                result = jnp.dot(left, right, preferred_element_type=F32)
                for at, place_x in enumerate(places):
                    lanes = slice(at * size, (at + 1) * size)
                    if start:
                        own[operator, place_n, place_x] = result[:size, lanes]
                    else:
                        own[operator, place_n, place_x] += result[:size, lanes]
                    prod[operator, number, place_n, place_x] = result[size:, lanes].astype(BF16)

    def own_row(number):
        @pl.loop(0, 2)
        def _(column):
            def load(operator, place):
                return a_own[operator, number, column, slot_of[1 + column, operator * 2 + number, place]]

            fine_rows(number, 1 + column, (0, 1), load)

    for copy in local:
        copy.wait()
    for column in (1, 2):
        table(
            column,
            lambda operator, number, slot, column=column: off_ref[operator, number, column - 1, slot],
            lambda operator, number, column=column: count_ref[operator, number, column - 1],
        )
    for turn in range(2):
        for side in range(2):
            wait_col(turn, (side,))
            row_copies[turn][1 + side].start()
        transposes(order[turn])
        if turn == 0:
            wait_col(6)
            wait_col(7)
            for side in range(2):
                halo_table(side)
    for copies in row_copies:
        for copy in copies:
            copy.wait_recv()

    prod_copies = [[], []]
    for turn in range(2):
        number = order[turn]
        own_row(number)
        for operator in range(2):
            for side, place_ns in ((1, (3, 4)), (0, (0, 1, 2))):
                half = halves[turn][operator][side]
                wait_col(2 + 2 * turn + operator, (side,))

                def load(operator, place):
                    return half[slot_of[3 * side, operator * 2 + number, place]]

                fine_rows(number, 3 * side, (operator,), load)
                products(operator, number, place_ns, turn == 0)
                part = slice(place_ns[0], place_ns[-1] + 1)
                copy = remote(
                    prod.at[operator, number, part], recv.at[operator, number, part],
                    prod_send.at[operator, turn, side], prod_recv.at[operator, number, side], to_row(number),
                )
                copy.start()
                prod_copies[operator].append(copy)

    for operator in range(2):
        for copy in prod_copies[operator]:
            copy.wait_recv()

        @pl.loop(0, 5)
        def _(place_n):
            for place in range(5):
                total = None
                if 1 <= place <= 3:
                    total = own[operator, place_n, place - 1]
                if place >= 2:
                    term = recv[operator, 0, place_n, place - 2].astype(F32)
                    total = term if total is None else total + term
                if place <= 2:
                    term = recv[operator, 1, place_n, place].astype(F32)
                    total = term if total is None else total + term
                out_ref[operator, place, place_n] = total.astype(BF16)

    for copies in col_copies + row_copies + prod_copies:
        for copy in copies:
            copy.wait_send()


def per_device(a_vals, a_off, a_count, p_vals):
    operators, size = a_vals.shape[0], a_vals.shape[-1]
    slots = a_vals.shape[3]
    rows, cols = lax.axis_size("row"), lax.axis_size("col")

    def body(*refs):
        kernel(rows, cols, *refs)

    block = (size, size)
    in_hbm = pl.BlockSpec(memory_space=pl.ANY)
    result = pl.pallas_call(
        body,
        out_shape=jax.ShapeDtypeStruct((operators, 5, 5) + block, BF16),
        in_specs=[in_hbm] * 4,
        out_specs=pl.BlockSpec(memory_space=pltpu.VMEM),
        scratch_shapes=[
            pltpu.VMEM((4, 6, 4) + block, BF16),
            pltpu.VMEM((2, 2, 2, slots + 1) + block, BF16),
        ]
        + [pltpu.VMEM((slots + 1,) + block, BF16)] * 8
        + [
            pltpu.SMEM(a_off.shape, jnp.int32),
            pltpu.SMEM(a_count.shape, jnp.int32),
            pltpu.SMEM((2,) + a_off.shape, jnp.int32),
            pltpu.SMEM((2,) + a_count.shape, jnp.int32),
            pltpu.SMEM((4, 8, 128), jnp.int32),
            pltpu.VMEM((2, 2, 4, 3, 3) + block, BF16),
            pltpu.VMEM((2, 2 * size, 4 * size), BF16),
            pltpu.VMEM((2, 5, 3) + block, F32),
            pltpu.VMEM((2, 2, 5, 3) + block, BF16),
            pltpu.VMEM((2, 2, 5, 3) + block, BF16),
            pltpu.SemaphoreType.DMA((4,)),
            pltpu.SemaphoreType.DMA((2, 8)),
            pltpu.SemaphoreType.DMA((2, 8)),
            pltpu.SemaphoreType.DMA((2, 3)),
            pltpu.SemaphoreType.DMA((2, 3)),
            pltpu.SemaphoreType.DMA((2, 2, 2)),
            pltpu.SemaphoreType.DMA((2, 2, 2)),
        ],
        compiler_params=pltpu.CompilerParams(
            collective_id=0, has_side_effects=True, vmem_limit_bytes=48 * 1024 * 1024
        ),
        name="galerkin",
    )(*[pltpu.with_memory_space_constraint(array, pltpu.HBM) for array in (a_vals, p_vals, a_off, a_count)])
    return result.reshape((operators, 1, 1, 25) + block)


def solution(mesh):
    placed = (
        P(None, "row", "col", None, None, None),
        P(None, "row", "col", None),
        P(None, "row", "col"),
        P("row", "col", None, None, None),
    )
    return jax.shard_map(
        per_device,
        mesh=mesh,
        in_specs=placed,
        out_specs=P(None, "row", "col", None, None, None),
        check_vma=False,
    )
```

```python
import jax
import jax.numpy as jnp
from jax import lax
from jax.experimental import pallas as pl
from jax.experimental.pallas import tpu as pltpu
from jax.sharding import PartitionSpec as P

MESH = pl.DeviceIdType.MESH
BF16 = jnp.bfloat16
F32 = jnp.float32

CORNER = {(-1, 0): 0, (-1, 1): 1, (0, 0): 1, (0, 1): 0, (1, 1): 0, (1, 2): 1}


def kernel(row_count, col_count, a_hbm, p_hbm, off_hbm, count_hbm, out_ref,
           p_win, a_own, a_0, a_1, a_2, a_3, a_4, a_5, a_6, a_7,
           off_ref, count_ref, off_halo, count_halo, slot_of,
           w_buf, lhs_t, own, prod, recv,
           local_sem, col_send, col_recv, row_send, row_recv, prod_send, prod_recv):
    r = lax.axis_index("row")
    c = lax.axis_index("col")
    rows = [lax.rem(r + row_count - 1, row_count), lax.rem(r + 1, row_count)]
    cols = [lax.rem(c + col_count - 1, col_count), lax.rem(c + 1, col_count)]
    first = lax.rem(r, 2)
    order = (first, 1 - first)
    halves = (((a_0, a_1), (a_2, a_3)), ((a_4, a_5), (a_6, a_7)))
    size = p_hbm.shape[-1]
    slots = a_hbm.shape[3]

    def to_row(number):
        return {"row": lax.rem(r + 2 * number - 1 + row_count, row_count), "col": c}

    barrier = pltpu.get_barrier_semaphore()
    for side in range(2):
        pl.semaphore_signal(barrier, inc=1, device_id={"row": rows[side], "col": c}, device_id_type=MESH)
        pl.semaphore_signal(barrier, inc=1, device_id={"row": r, "col": cols[side]}, device_id_type=MESH)

    local = [
        pltpu.make_async_copy(p_hbm, p_win.at[1:3, 2:4], local_sem.at[0]),
        pltpu.make_async_copy(a_hbm, a_own.at[:, :, :, 0:slots], local_sem.at[1]),
        pltpu.make_async_copy(off_hbm, off_ref, local_sem.at[2]),
        pltpu.make_async_copy(count_hbm, count_ref, local_sem.at[3]),
    ]
    for copy in local:
        copy.start()
    pl.semaphore_wait(barrier, 4)

    def remote(src, dst, send, recv_s, device):
        return pltpu.make_async_remote_copy(
            src_ref=src, dst_ref=dst, send_sem=send, recv_sem=recv_s,
            device_id=device, device_id_type=MESH,
        )

    col_copies = [[], []]
    for side in range(2):
        device = {"row": r, "col": cols[side]}
        land = 1 - side
        near = side
        at = 0 if land == 0 else 4
        parts = [(p_hbm.at[number], p_win.at[1 + number, at : at + 2]) for number in order]
        for turn in range(2):
            for operator in range(2):
                parts.append(
                    (a_hbm.at[operator, order[turn], near], halves[turn][operator][land].at[0:slots])
                )
        parts.append((off_hbm, off_halo.at[land]))
        parts.append((count_hbm, count_halo.at[land]))
        for part, (src, dst) in enumerate(parts):
            col_copies[side].append(
                remote(src, dst, col_send.at[side, part], col_recv.at[land, part], device)
            )
    row_copies = [[], []]
    for turn in range(2):
        number = order[turn]
        row_at = 3 * (1 - number)
        parts = [(p_hbm.at[number], p_win.at[row_at, 2:4])]
        for at in (0, 4):
            parts.append((p_win.at[1 + number, at : at + 2], p_win.at[row_at, at : at + 2]))
        for part, (src, dst) in enumerate(parts):
            row_copies[turn].append(
                remote(src, dst, row_send.at[turn, part], row_recv.at[number, part], to_row(number))
            )

    def start_col(part):
        for side in range(2):
            col_copies[side][part].start()

    def wait_col(part, sides=(0, 1)):
        for side in sides:
            col_copies[1 - side][part].wait_recv()

    start_col(0)
    for turn in range(2):
        row_copies[turn][0].start()
    for part in (6, 7, 1, 2, 3, 4, 5):
        start_col(part)

    zero = jnp.zeros((size, size), BF16)
    for operator in range(2):
        for side in range(2):
            for turn in range(2):
                halves[turn][operator][side][slots] = zero
                a_own[operator, turn, side, slots] = zero

    def table(column, off_at, count_at):
        @pl.loop(0, 4)
        def _(line):
            operator = line // 2
            number = lax.rem(line, 2)
            flip_x = 1 - 2 * number
            flip_y = 2 * (column % 2) - 1
            count = count_at(operator, number)
            places = []
            for slot in range(slots):
                off = off_at(operator, number, slot)
                off_x = (off >= 3).astype(jnp.int32) + (off >= 6).astype(jnp.int32)
                off_y = off - 3 * off_x
                place = 3 * (flip_x * (off_x - 1) + 1) + flip_y * (off_y - 1) + 1
                places.append(jnp.where(slot < count, place, -1))
            for position in range(9):
                found = jnp.int32(slots)
                for slot in range(slots):
                    found = jnp.where(places[slot] == position, slot, found)
                slot_of[column, line, position] = found

    def halo_table(side):
        table(
            3 * side,
            lambda operator, number, slot: off_halo[side, operator, number, 1 - side, slot],
            lambda operator, number: count_halo[side, operator, number, 1 - side],
        )

    def fine_rows(number, column, operators, load):
        flip_x = 1 - 2 * number
        flip_y = 2 * (column % 2) - 1

        def p_block(off_x, off_y, corner_x, corner_y):
            return p_win[number + 1 + flip_x * off_x, column + 1 + flip_y * off_y, 2 * corner_x + corner_y]

        for place_x in range(3):
            offs_x = [off for off in (-1, 0, 1) if (off, place_x) in CORNER]
            results = []
            for offs_y, places_y in (((-1, 0), (0, 1)), ((1,), (1, 2))):
                pairs = [(off_x, off_y) for off_x in offs_x for off_y in offs_y]
                left = jnp.concatenate(
                    [
                        jnp.concatenate(
                            [load(operator, (off_x + 1) * 3 + off_y + 1) for operator in operators], axis=0
                        )
                        for off_x, off_y in pairs
                    ],
                    axis=1,
                )
                right = jnp.concatenate(
                    [
                        jnp.concatenate(
                            [
                                p_block(off_x, off_y, CORNER[off_x, place_x], CORNER[off_y, place_y])
                                for place_y in places_y
                            ],
                            axis=1,
                        )
                        for off_x, off_y in pairs
                    ],
                    axis=0,
                )
                results.append(jnp.dot(left, right, preferred_element_type=F32))
            low, high = results
            columns = [low[:, :size], low[:, size:] + high[:, :size], high[:, size:]]
            for place_y in range(3):
                for at, operator in enumerate(operators):
                    w_buf[operator, number, column, 1 + flip_x * (place_x - 1), 1 + flip_y * (place_y - 1)] = (
                        columns[place_y][at * size : (at + 1) * size].astype(BF16)
                    )

    def transposes(number):
        for column in range(4):
            corner_y = 1 if column in (0, 3) else 0
            for corner_x in range(2):
                lhs_t[number, corner_x * size : (corner_x + 1) * size, column * size : (column + 1) * size] = p_win[
                    1 + number, column + 1, 2 * corner_x + corner_y
                ].T

    def products(operator, number, place_ns, start):
        for place_n in place_ns:
            low = [0, 0, 0, 1, 3][place_n]
            high = [1, 3, 4, 4, 4][place_n]
            left = lhs_t[number, :, low * size : high * size]
            for places in ((0, 1), (2,)):
                right = jnp.concatenate(
                    [
                        jnp.concatenate(
                            [
                                w_buf[operator, number, column, place_x, place_n - [0, 1, 1, 2][column]]
                                for place_x in places
                            ],
                            axis=1,
                        )
                        for column in range(low, high)
                    ],
                    axis=0,
                )
                result = jnp.dot(left, right, preferred_element_type=F32)
                for at, place_x in enumerate(places):
                    lanes = slice(at * size, (at + 1) * size)
                    if start:
                        own[operator, place_n, place_x] = result[:size, lanes]
                    else:
                        own[operator, place_n, place_x] += result[:size, lanes]
                    prod[operator, number, place_n, place_x] = result[size:, lanes].astype(BF16)

    def own_row(number):
        @pl.loop(0, 2)
        def _(column):
            def load(operator, place):
                return a_own[operator, number, column, slot_of[1 + column, operator * 2 + number, place]]

            fine_rows(number, 1 + column, (0, 1), load)

    for copy in local:
        copy.wait()
    for column in (1, 2):
        table(
            column,
            lambda operator, number, slot, column=column: off_ref[operator, number, column - 1, slot],
            lambda operator, number, column=column: count_ref[operator, number, column - 1],
        )
    for turn in range(2):
        for side in range(2):
            wait_col(turn, (side,))
            row_copies[turn][1 + side].start()
        transposes(order[turn])
        if turn == 0:
            wait_col(6)
            wait_col(7)
            for side in range(2):
                halo_table(side)
    for copies in row_copies:
        for copy in copies:
            copy.wait_recv()

    prod_copies = [[], []]
    for turn in range(2):
        number = order[turn]
        if turn == 0:
            own_row(number)
        for operator in range(2):
            for side, place_ns in ((1, (3, 4)), (0, (0, 1, 2))):
                half = halves[turn][operator][side]
                wait_col(2 + 2 * turn + operator, (side,))

                def load(operator, place):
                    return half[slot_of[3 * side, operator * 2 + number, place]]

                fine_rows(number, 3 * side, (operator,), load)
                products(operator, number, place_ns, turn == 0)
                part = slice(place_ns[0], place_ns[-1] + 1)
                copy = remote(
                    prod.at[operator, number, part], recv.at[operator, number, part],
                    prod_send.at[operator, turn, side], prod_recv.at[operator, number, side], to_row(number),
                )
                copy.start()
                prod_copies[operator].append(copy)
            if turn == 0 and operator == 0:
                own_row(order[1])

    for operator in range(2):
        for copy in prod_copies[operator]:
            copy.wait_recv()

        @pl.loop(0, 5)
        def _(place_n):
            for place in range(5):
                total = None
                if 1 <= place <= 3:
                    total = own[operator, place_n, place - 1]
                if place >= 2:
                    term = recv[operator, 0, place_n, place - 2].astype(F32)
                    total = term if total is None else total + term
                if place <= 2:
                    term = recv[operator, 1, place_n, place].astype(F32)
                    total = term if total is None else total + term
                out_ref[operator, place, place_n] = total.astype(BF16)

    for copies in col_copies + row_copies + prod_copies:
        for copy in copies:
            copy.wait_send()


def per_device(a_vals, a_off, a_count, p_vals):
    operators, size = a_vals.shape[0], a_vals.shape[-1]
    slots = a_vals.shape[3]
    rows, cols = lax.axis_size("row"), lax.axis_size("col")

    def body(*refs):
        kernel(rows, cols, *refs)

    block = (size, size)
    in_hbm = pl.BlockSpec(memory_space=pl.ANY)
    result = pl.pallas_call(
        body,
        out_shape=jax.ShapeDtypeStruct((operators, 5, 5) + block, BF16),
        in_specs=[in_hbm] * 4,
        out_specs=pl.BlockSpec(memory_space=pltpu.VMEM),
        scratch_shapes=[
            pltpu.VMEM((4, 6, 4) + block, BF16),
            pltpu.VMEM((2, 2, 2, slots + 1) + block, BF16),
        ]
        + [pltpu.VMEM((slots + 1,) + block, BF16)] * 8
        + [
            pltpu.SMEM(a_off.shape, jnp.int32),
            pltpu.SMEM(a_count.shape, jnp.int32),
            pltpu.SMEM((2,) + a_off.shape, jnp.int32),
            pltpu.SMEM((2,) + a_count.shape, jnp.int32),
            pltpu.SMEM((4, 8, 128), jnp.int32),
            pltpu.VMEM((2, 2, 4, 3, 3) + block, BF16),
            pltpu.VMEM((2, 2 * size, 4 * size), BF16),
            pltpu.VMEM((2, 5, 3) + block, F32),
            pltpu.VMEM((2, 2, 5, 3) + block, BF16),
            pltpu.VMEM((2, 2, 5, 3) + block, BF16),
            pltpu.SemaphoreType.DMA((4,)),
            pltpu.SemaphoreType.DMA((2, 8)),
            pltpu.SemaphoreType.DMA((2, 8)),
            pltpu.SemaphoreType.DMA((2, 3)),
            pltpu.SemaphoreType.DMA((2, 3)),
            pltpu.SemaphoreType.DMA((2, 2, 2)),
            pltpu.SemaphoreType.DMA((2, 2, 2)),
        ],
        compiler_params=pltpu.CompilerParams(
            collective_id=0, has_side_effects=True, vmem_limit_bytes=48 * 1024 * 1024,
        ),
        name="galerkin",
    )(*[pltpu.with_memory_space_constraint(array, pltpu.HBM) for array in (a_vals, p_vals, a_off, a_count)])
    return result.reshape((operators, 1, 1, 25) + block)


def solution(mesh):
    placed = (
        P(None, "row", "col", None, None, None),
        P(None, "row", "col", None),
        P(None, "row", "col"),
        P("row", "col", None, None, None),
    )
    return jax.shard_map(
        per_device,
        mesh=mesh,
        in_specs=placed,
        out_specs=P(None, "row", "col", None, None, None),
        check_vma=False,
    )
```
